32 devices in a mesh: parts: 2 (over y), lon: 4 (over z), lat: 2 (over core), chan: 2 (over x).
Axes of the slice: x: 2, y: 2, z: 4, core: 2. Of those that a mesh axis runs over, the one named last changes fastest.
Arguments:
- fine_act: bfloat16 [384, 896, 256], P(('parts', 'lat', 'chan'), 'lon'), parts along dimension 0, may hold values from -6 to 6
- coarse_grad: bfloat16 [192, 448, 128], P(('parts', 'lat'), 'lon', 'chan'), parts along dimension 0, may hold values from -6 to 6
- kernel: bfloat16 [3, 3, 256, 128], replicated, may hold values from -0.125 to 0.125
Outputs:
- input_grad: bfloat16 [384, 896, 256], P(('parts', 'lat', 'chan'), 'lon'), parts along dimension 0
- kernel_grad: float32 [6, 3, 256, 128], P('parts'), parts along dimension 0
The draws below stay inside these ranges and needn't reach their ends.
There are 2 independent parts, one for each index of `parts`. The reference program is written for one: setup_inputs(seed, part) draws one part's arguments, and reference() takes and returns one part's arrays. A program takes and returns all parts, laid end to end along the dimension named above; an argument that names none is the same for every part. Nothing has to cross between parts.
All inputs are finite; a program needn't handle non-finite values.
Results may differ from the reference program's by a relative error of at most 0.001.
Values may be sent and summed in bfloat16 or wider, within the bound.
A program may use at most 64 MiB of HBM per device.

```python
import math
import jax
import jax.numpy as jnp

CIN = 256
COUT = 128
NLAT = 192
NLON = 896
CLAT = 96
CLON = 448


def levels(rng, extent, cuts, smallest, largest):
    loudness = 1.0
    for position, blocks in cuts:
        draws = jax.random.uniform(jax.random.fold_in(jax.random.fold_in(rng, 6), position), (blocks,), jnp.float32, smallest / len(cuts), largest / len(cuts))
        loudness = loudness * jnp.repeat(jnp.exp(draws), extent[position] // blocks).reshape((-1,) + (1,) * (len(extent) - 1 - position))
    return loudness


def scatter_about(rng, extent, width, bound, split=(), dtype=jnp.bfloat16):
    factor_of = levels(rng, extent, split, -0.22, 0.18) if split else 1.0
    values = jax.random.normal(rng, extent, jnp.float32) * width * factor_of
    return jnp.minimum(jnp.maximum(values, -bound), bound).astype(dtype)


def setup_inputs(seed: int = 0, part: int = 0) -> dict:
    key_list = jax.random.split(jax.random.key(seed), 4)
    part_keys = jax.random.split(jax.random.fold_in(key_list[3], part), 4)
    return {
        "fine_act": scatter_about(part_keys[0], (NLAT, NLON, CIN), 1.0, 6.0, ((0, 4), (1, 4))),
        "coarse_grad": scatter_about(part_keys[1], (CLAT, CLON, COUT), 1.0, 6.0, ((0, 2), (1, 4), (2, 2))),
        "kernel": scatter_about(key_list[2], (3, 3, CIN, COUT), (9 * CIN) ** -0.5, 0.125),
    }


def reference(fine_act, coarse_grad, kernel):
    even_act = fine_act[::2, ::2, :]
    even_flat = even_act.reshape(CLAT * CLON, CIN)
    padded = jnp.pad(coarse_grad, ((1, 1), (0, 0), (0, 0)))
    padded = jnp.concatenate([padded[:, -1:], padded, padded[:, :1]], axis=1)
    total = jnp.zeros((CLAT * CLON, CIN), jnp.float32)
    partial_list = []
    for tap_row in range(3):
        for tap_col in range(3):
            shifted = padded[2 - tap_row:2 - tap_row + CLAT, 2 - tap_col:2 - tap_col + CLON].reshape(CLAT * CLON, COUT)
            total = total + jnp.dot(shifted, kernel[tap_row, tap_col].T, preferred_element_type=jnp.float32)
            partial_list.append(jnp.dot(even_flat.T, shifted, preferred_element_type=jnp.float32))
    even_grad = total.astype(jnp.bfloat16).reshape(CLAT, CLON, CIN)
    input_grad = jnp.zeros((NLAT, NLON, CIN), jnp.bfloat16).at[::2, ::2, :].set(even_grad)
    kernel_grad = jnp.stack(partial_list).reshape(3, 3, CIN, COUT) * (1.0 / math.sqrt(CLAT * CLON))
    return (input_grad, kernel_grad)
```

```python
import functools
import math

import jax
import jax.numpy as jnp
from jax import lax
from jax.experimental import pallas as pl
from jax.experimental.pallas import tpu as pltpu
from jax.sharding import PartitionSpec as P

MESH = pl.DeviceIdType.MESH
LANES = 128
F32 = jnp.float32
BF16 = jnp.bfloat16
AXES = ("lon", "lat", "chan")


def one_hot(shape, test):
    rows = lax.broadcasted_iota(jnp.int32, shape, 0)
    cols = lax.broadcasted_iota(jnp.int32, shape, 1)
    return jnp.where(test(rows, cols), 1.0, 0.0).astype(BF16)


def share(rows, peers, unit):
    for size in range(unit, rows + 1, unit):
        if rows % size == 0 and rows // size <= peers:
            return size
    raise ValueError("no share")


def stage_plan(rows, order, sizes):
    plan = []
    for position, axis in enumerate(order):
        unit = 8
        for later in order[position + 1:]:
            unit *= sizes[later] if later != "lon" else 1
        part = share(rows, sizes[axis], unit)
        plan.append((axis, part, rows // part))
        rows = part
    return plan


def grads_kernel(
    sizes, half_rows, half_cols, out_ch, scale,
    fine, cg, kernel, eg_out, kg_out,
    fbuf, kcat, tiles, taps, even_t, edge_out, edge_in, acc, *rest,
):
    landing, (local_sem, tile_recv, tile_send, edge_send, edge_recv, red_send, red_recv, gat_send, gat_recv) = rest[:-9], rest[-9:]
    lon_n, lat_n, chan_n = (sizes[a] for a in AXES)
    me = {a: lax.axis_index(a) for a in AXES}
    lat, chan = me["lat"], me["chan"]
    h = half_rows
    width = cg.shape[1]
    in_ch = fbuf.shape[2]
    mine = pl.ds(pl.multiple_of(chan * width, width), width)

    def other(axis, step):
        return lax.rem(me[axis] + step, sizes[axis])

    local = [pltpu.make_async_copy(fine.at[:, 0], fbuf, local_sem.at[0])]
    for r in range(3):
        for s in range(3):
            local.append(
                pltpu.make_async_copy(
                    kernel.at[r, s], kcat.at[r, :, pl.ds(s * out_ch, out_ch)], local_sem.at[1 + 3 * r + s]
                )
            )
    for copy in local:
        copy.start()

    is_top = jnp.logical_and(lat == 0, chan == 0)
    is_bottom = jnp.logical_and(lat == lat_n - 1, chan == chan_n - 1)
    pltpu.make_async_copy(cg.at[pl.ds(chan * h, h)], tiles.at[pl.ds(1, h), mine], tile_recv.at[2]).start()

    @pl.when(chan > 0)
    def _():
        pltpu.make_async_copy(cg.at[chan * h - 1], tiles.at[0, mine], tile_recv.at[0]).start()

    @pl.when(chan < chan_n - 1)
    def _():
        pltpu.make_async_copy(cg.at[(chan + 1) * h], tiles.at[h + 1, mine], tile_recv.at[1]).start()

    barrier = pltpu.get_barrier_semaphore()
    greeted = 0
    for dl in range(lat_n):
        for dc in range(chan_n):
            if dl or dc:
                pl.semaphore_signal(
                    barrier, inc=1, device_id={"lat": other("lat", dl), "chan": other("chan", dc)}, device_id_type=MESH
                )
                greeted += 1
    for d in range(1, lon_n):
        pl.semaphore_signal(barrier, inc=1, device_id={"lon": other("lon", d)}, device_id_type=MESH)
        greeted += 1
    pl.semaphore_wait(barrier, greeted)

    sends = []

    def send(condition, src, dst, send_sem, recv_sem, where):
        copy = pltpu.make_async_remote_copy(
            src_ref=src, dst_ref=dst, send_sem=send_sem, recv_sem=recv_sem, device_id=where, device_id_type=MESH
        )
        if condition is None:
            copy.start()
        else:
            pl.when(condition)(lambda: copy.start())
        sends.append((condition, copy))

    slot = 0
    for d in range(1, chan_n):
        p = other("chan", d)
        send(p > 0, cg.at[jnp.maximum(p * h - 1, 0)], tiles.at[0, mine], tile_send.at[slot], tile_recv.at[0], {"chan": p})
        send(None, cg.at[pl.ds(p * h, h)], tiles.at[pl.ds(1, h), mine], tile_send.at[slot + 1], tile_recv.at[2], {"chan": p})
        send(
            p < chan_n - 1, cg.at[jnp.minimum((p + 1) * h, chan_n * h - 1)], tiles.at[h + 1, mine],
            tile_send.at[slot + 2], tile_recv.at[1], {"chan": p},
        )
        slot += 3
    send(
        lat < lat_n - 1, cg.at[chan_n * h - 1], tiles.at[0, mine], tile_send.at[slot], tile_recv.at[0],
        {"lat": jnp.minimum(lat + 1, lat_n - 1), "chan": 0},
    )
    send(
        lat > 0, cg.at[0], tiles.at[h + 1, mine], tile_send.at[slot + 1], tile_recv.at[1],
        {"lat": jnp.maximum(lat - 1, 0), "chan": chan_n - 1},
    )

    local[0].wait()
    pick = one_hot((2 * half_cols, LANES), lambda row, col: row == 2 * col)

    def take_even(i, _):
        picked = lax.dot_general(fbuf[i], pick, (((0,), (0,)), ((), ())), preferred_element_type=F32)
        even_t[:, pl.ds(pl.multiple_of(i * LANES, LANES), LANES)] = picked.astype(BF16)
        return 0

    lax.fori_loop(0, h, take_even, 0)

    @pl.when(is_top)
    def _():
        tiles[0] = jnp.zeros(tiles.shape[1:], BF16)

    @pl.when(is_bottom)
    def _():
        tiles[h + 1] = jnp.zeros(tiles.shape[1:], BF16)

    @pl.when(jnp.logical_not(is_top))
    def _():
        pltpu.make_async_copy(tiles.at[0], tiles.at[0], tile_recv.at[0]).wait()

    @pl.when(jnp.logical_not(is_bottom))
    def _():
        pltpu.make_async_copy(tiles.at[h + 1], tiles.at[h + 1], tile_recv.at[1]).wait()

    pltpu.make_async_copy(tiles.at[pl.ds(1, h)], tiles.at[pl.ds(1, h)], tile_recv.at[2]).wait()

    def shifted_source(row, col):
        s, j = col // LANES, col % LANES
        return jnp.logical_and(row == j + 1 - s, j < half_cols)

    shift = one_hot((half_cols, 3 * LANES), shifted_source)

    def build(k, edges):
        tile = tiles[k]
        moved = jnp.dot(tile, shift, preferred_element_type=F32).astype(BF16)
        at = pl.ds(pl.multiple_of(k * LANES, LANES), LANES)
        for s in range(3):
            taps[pl.ds(s * out_ch, out_ch), at] = moved[:, s * LANES:(s + 1) * LANES]
        last = one_hot(
            (half_cols, 2 * LANES),
            lambda row, col: jnp.logical_or(
                jnp.logical_and(row == half_cols - 1, col == k), jnp.logical_and(row == 0, col == k + LANES)
            ),
        )
        return edges + jnp.dot(tile, last, preferred_element_type=F32)

    edges = lax.fori_loop(0, h + 2, build, jnp.zeros((out_ch, 2 * LANES), F32)).astype(BF16)
    edge_out[0] = edges[:, :LANES]
    edge_out[1] = edges[:, LANES:]
    send(None, edge_out.at[0], edge_in.at[0], edge_send.at[0], edge_recv.at[0], {"lon": other("lon", 1)})
    send(None, edge_out.at[1], edge_in.at[1], edge_send.at[1], edge_recv.at[1], {"lon": other("lon", lon_n - 1)})
    for side in range(2):
        pltpu.make_async_copy(edge_in.at[side], edge_in.at[side], edge_recv.at[side]).wait()

    def inject(k, _):
        at = pl.ds(pl.multiple_of(k * LANES, LANES), LANES)
        for side, s, lane in ((1, 0, half_cols - 1), (0, 2, 0)):
            spot = one_hot((LANES, LANES), lambda row, col: jnp.logical_and(row == k, col == lane))
            block = taps[pl.ds(s * out_ch, out_ch), at].astype(F32)
            block = block + jnp.dot(edge_in[side], spot, preferred_element_type=F32)
            taps[pl.ds(s * out_ch, out_ch), at] = block.astype(BF16)
        return 0

    lax.fori_loop(0, h + 2, inject, 0)

    for r in range(3):
        part = lax.dot_general(
            even_t[...], taps[:, (2 - r) * LANES:(2 - r + h) * LANES], (((1,), (1,)), ((), ())), preferred_element_type=F32
        )
        for s in range(3):
            acc[pl.ds((3 * r + s) * in_ch, in_ch), :] = part[:, s * out_ch:(s + 1) * out_ch]

    streams = reduce_streams(acc.shape[0], sizes)
    bases = [base for base, _ in streams]
    stacks = [[] for _ in streams]
    counter = {"red": 0, "gat": 0, "land": 0}

    def started(stage):
        begun = []
        for index, (_, plan) in enumerate(streams):
            axis, part, owners = plan[stage]
            base = bases[index]
            land = landing[counter["land"]]
            counter["land"] += 1
            amowner = me[axis] < owners if owners < sizes[axis] else None
            arrivals = []
            for d in range(1, sizes[axis]):
                p = other(axis, d)
                n = counter["red"]
                counter["red"] += 1
                toowner = p < owners if owners < sizes[axis] else None
                target = p if toowner is None else jnp.minimum(p, owners - 1)
                send(
                    toowner, acc.at[pl.ds(pl.multiple_of(base + target * part, 8), part)], land.at[d - 1],
                    red_send.at[n], red_recv.at[n], {axis: p},
                )
                arrivals.append(n)
            own = me[axis] if amowner is None else jnp.minimum(me[axis], owners - 1)
            bases[index] = base + own * part
            stacks[index].append((axis, part, owners, base, amowner))
            begun.append((index, land, arrivals, amowner, part))
        return begun

    def finished(begun, final):
        for index, land, arrivals, amowner, part in begun:
            at = pl.ds(pl.multiple_of(bases[index], 8), part)

            def absorb():
                for position, n in enumerate(arrivals):
                    pltpu.make_async_copy(land.at[position], land.at[position], red_recv.at[n]).wait()
                total = acc[at, :]
                for position in range(len(arrivals)):
                    total = total + land[position]
                if final:
                    kg_out[at, :] = total * scale
                else:
                    acc[at, :] = total

            if amowner is None:
                absorb()
            else:
                pl.when(amowner)(absorb)

    begun = started(0)
    finished(begun, False)
    begun = started(1)

    for copy in local[1:]:
        copy.wait()

    def make_even_grad(i, _):
        total = jnp.zeros((in_ch, 2 * LANES), F32)
        for r in range(3):
            at = pl.ds(pl.multiple_of(i * 2 * LANES + (2 - r) * LANES, LANES), 2 * LANES)
            total = total + jnp.dot(kcat[r], taps[:, at], preferred_element_type=F32)
        eg_out[:, pl.ds(pl.multiple_of(i * 2 * LANES, LANES), 2 * LANES)] = total.astype(BF16)
        return 0

    lax.fori_loop(0, h // 2, make_even_grad, 0)

    finished(begun, False)
    begun = started(2)
    finished(begun, True)

    for stage in (2, 1, 0):
        waits = []
        for index in range(len(streams)):
            axis, part, owners, base, amowner = stacks[index][stage]
            own = me[axis] if amowner is None else jnp.minimum(me[axis], owners - 1)
            at = pl.ds(pl.multiple_of(base + own * part, 8), part)
            for d in range(1, sizes[axis]):
                n = counter["gat"]
                counter["gat"] += 1
                send(amowner, kg_out.at[at], kg_out.at[at], gat_send.at[n], gat_recv.at[n], {axis: other(axis, d)})
                q = other(axis, sizes[axis] - d)
                fromowner = q < owners if owners < sizes[axis] else None
                source = q if fromowner is None else jnp.minimum(q, owners - 1)
                there = kg_out.at[pl.ds(pl.multiple_of(base + source * part, 8), part)]
                waits.append((fromowner, pltpu.make_async_copy(there, there, gat_recv.at[n])))
        for condition, copy in waits:
            if condition is None:
                copy.wait()
            else:
                pl.when(condition)(lambda copy=copy: copy.wait())

    for condition, copy in sends:
        if condition is None:
            copy.wait_send()
        else:
            pl.when(condition)(lambda copy=copy: copy.wait_send())


def reduce_streams(rows, sizes):
    half = rows // sizes["lat"] // 2
    streams = []
    for index, order in enumerate((("lon", "chan"), ("chan", "lon"))):
        plan = [("lat", half, sizes["lat"])] + stage_plan(half, order, sizes)
        streams.append((index * half * sizes["lat"], plan))
    return streams


def spread_kernel(half_cols, eg, out):
    spread = one_hot((2 * half_cols, LANES), lambda row, col: row == 2 * col)
    for k in range(out.shape[0] // 2):
        row = lax.dot_general(
            spread, eg[:, k * LANES:(k + 1) * LANES], (((1,), (1,)), ((), ())), preferred_element_type=F32
        )
        out[2 * k] = row.astype(BF16)
        out[2 * k + 1] = jnp.zeros(out.shape[1:], BF16)


def on_device(sizes, fine_act, coarse_grad, kernel):
    fine_rows, fine_cols, in_ch = fine_act.shape
    out_ch = kernel.shape[3]
    h, w = fine_rows // 2, fine_cols // 2
    lon_n, lat_n, chan_n = (sizes[a] for a in AXES)
    scale = 1.0 / math.sqrt(h * lat_n * chan_n * w * lon_n)
    cg = jnp.transpose(coarse_grad, (0, 2, 1))
    fine = fine_act.reshape(h, 2, fine_cols, in_ch)
    streams = reduce_streams(9 * in_ch, sizes)
    landing, count = [], 0
    for stage in range(3):
        for _, plan in streams:
            axis, part, _ = plan[stage]
            landing.append(pltpu.VMEM((sizes[axis] - 1, part, out_ch), F32))
            count += sizes[axis] - 1
    dma = pltpu.SemaphoreType.DMA
    vmem = pl.BlockSpec(memory_space=pltpu.VMEM)
    hbm = pl.BlockSpec(memory_space=pl.ANY)
    eg, kg = pl.pallas_call(
        functools.partial(grads_kernel, sizes, h, w, out_ch, scale),
        out_shape=(
            jax.ShapeDtypeStruct((in_ch, h * LANES), BF16),
            jax.ShapeDtypeStruct((9 * in_ch, out_ch), F32),
        ),
        in_specs=[hbm, hbm, hbm],
        out_specs=(vmem, vmem),
        scratch_shapes=[
            pltpu.VMEM((h, fine_cols, in_ch), BF16),
            pltpu.VMEM((3, in_ch, 3 * out_ch), BF16),
            pltpu.VMEM((h + 2, out_ch, w), BF16),
            pltpu.VMEM((3 * out_ch, (h + 2) * LANES), BF16),
            pltpu.VMEM((in_ch, h * LANES), BF16),
            pltpu.VMEM((2, out_ch, LANES), BF16),
            pltpu.VMEM((2, out_ch, LANES), BF16),
            pltpu.VMEM((9 * in_ch, out_ch), F32),
            *landing,
            dma((10,)),
            dma((3,)),
            dma((3 * (chan_n - 1) + 2,)),
            dma((2,)),
            dma((2,)),
            dma((count,)),
            dma((count,)),
            dma((count,)),
            dma((count,)),
        ],
        compiler_params=pltpu.CompilerParams(
            collective_id=0, has_side_effects=True, vmem_limit_bytes=40 * 1024 * 1024
        ),
        name="grads",
    )(fine, cg, kernel)
    step = 4 if h % 4 == 0 else 1
    input_grad = pl.pallas_call(
        functools.partial(spread_kernel, w),
        out_shape=jax.ShapeDtypeStruct(fine_act.shape, BF16),
        grid=(h // step,),
        in_specs=[pl.BlockSpec((in_ch, step * LANES), lambda i: (0, i))],
        out_specs=pl.BlockSpec((2 * step, fine_cols, in_ch), lambda i: (i, 0, 0)),
        name="spread",
    )(eg)
    return (input_grad, kg.reshape(3, 3, in_ch, out_ch))


def solution(mesh):
    placed = (P(("parts", "lat", "chan"), "lon", None), P(("parts", "lat"), "lon", "chan"), P())
    sizes = {axis: mesh.shape[axis] for axis in AXES}
    return jax.shard_map(
        functools.partial(on_device, sizes),
        mesh=mesh,
        in_specs=placed,
        out_specs=(P(("parts", "lat", "chan"), "lon", None), P("parts", None, None, None)),
        check_vma=False,
    )
```

```python
import functools
import math

import jax
import jax.numpy as jnp
from jax import lax
from jax.experimental import pallas as pl
from jax.experimental.pallas import tpu as pltpu
from jax.sharding import PartitionSpec as P

MESH = pl.DeviceIdType.MESH
LANES = 128
F32 = jnp.float32
BF16 = jnp.bfloat16
AXES = ("lon", "lat", "chan")


def one_hot(shape, test):
    rows = lax.broadcasted_iota(jnp.int32, shape, 0)
    cols = lax.broadcasted_iota(jnp.int32, shape, 1)
    return jnp.where(test(rows, cols), 1.0, 0.0).astype(BF16)


def share(rows, peers, unit):
    for size in range(unit, rows + 1, unit):
        if rows % size == 0 and rows // size <= peers:
            return size
    raise ValueError("no share")


def stage_plan(rows, order, sizes):
    plan = []
    for position, axis in enumerate(order):
        unit = 8
        for later in order[position + 1:]:
            unit *= sizes[later] if later != "lon" else 1
        part = share(rows, sizes[axis], unit)
        plan.append((axis, part, rows // part))
        rows = part
    return plan


def grads_kernel(
    sizes, half_rows, half_cols, out_ch, scale,
    fine, cg, kernel, rows_out, kg_out,
    fbuf, kcat, tiles, taps, even_t, edge_out, edge_in, acc, rows_buf, row_sem, *rest,
):
    landing, (local_sem, tile_recv, tile_send, edge_send, edge_recv, red_send, red_recv, gat_send, gat_recv) = rest[:-9], rest[-9:]
    lon_n, lat_n, chan_n = (sizes[a] for a in AXES)
    me = {a: lax.axis_index(a) for a in AXES}
    lat, chan = me["lat"], me["chan"]
    h = half_rows
    width = cg.shape[1]
    in_ch = fbuf.shape[2]
    mine = pl.ds(pl.multiple_of(chan * width, width), width)

    def other(axis, step):
        return lax.rem(me[axis] + step, sizes[axis])

    local = [pltpu.make_async_copy(fine.at[:, 0], fbuf, local_sem.at[0])]
    for r in range(3):
        for s in range(3):
            local.append(
                pltpu.make_async_copy(
                    kernel.at[r, s], kcat.at[r, :, pl.ds(s * out_ch, out_ch)], local_sem.at[1 + 3 * r + s]
                )
            )
    for copy in local:
        copy.start()

    is_top = jnp.logical_and(lat == 0, chan == 0)
    is_bottom = jnp.logical_and(lat == lat_n - 1, chan == chan_n - 1)
    pltpu.make_async_copy(cg.at[pl.ds(chan * h, h)], tiles.at[pl.ds(1, h), mine], tile_recv.at[2]).start()

    @pl.when(chan > 0)
    def _():
        pltpu.make_async_copy(cg.at[chan * h - 1], tiles.at[0, mine], tile_recv.at[0]).start()

    @pl.when(chan < chan_n - 1)
    def _():
        pltpu.make_async_copy(cg.at[(chan + 1) * h], tiles.at[h + 1, mine], tile_recv.at[1]).start()

    barrier = pltpu.get_barrier_semaphore()
    greeted = 0
    for dl in range(lat_n):
        for dc in range(chan_n):
            if dl or dc:
                pl.semaphore_signal(
                    barrier, inc=1, device_id={"lat": other("lat", dl), "chan": other("chan", dc)}, device_id_type=MESH
                )
                greeted += 1
    for d in range(1, lon_n):
        pl.semaphore_signal(barrier, inc=1, device_id={"lon": other("lon", d)}, device_id_type=MESH)
        greeted += 1
    pl.semaphore_wait(barrier, greeted)

    sends = []

    def send(condition, src, dst, send_sem, recv_sem, where):
        copy = pltpu.make_async_remote_copy(
            src_ref=src, dst_ref=dst, send_sem=send_sem, recv_sem=recv_sem, device_id=where, device_id_type=MESH
        )
        if condition is None:
            copy.start()
        else:
            pl.when(condition)(lambda: copy.start())
        sends.append((condition, copy))

    slot = 0
    for d in range(1, chan_n):
        p = other("chan", d)
        send(p > 0, cg.at[jnp.maximum(p * h - 1, 0)], tiles.at[0, mine], tile_send.at[slot], tile_recv.at[0], {"chan": p})
        send(None, cg.at[pl.ds(p * h, h)], tiles.at[pl.ds(1, h), mine], tile_send.at[slot + 1], tile_recv.at[2], {"chan": p})
        send(
            p < chan_n - 1, cg.at[jnp.minimum((p + 1) * h, chan_n * h - 1)], tiles.at[h + 1, mine],
            tile_send.at[slot + 2], tile_recv.at[1], {"chan": p},
        )
        slot += 3
    send(
        lat < lat_n - 1, cg.at[chan_n * h - 1], tiles.at[0, mine], tile_send.at[slot], tile_recv.at[0],
        {"lat": jnp.minimum(lat + 1, lat_n - 1), "chan": 0},
    )
    send(
        lat > 0, cg.at[0], tiles.at[h + 1, mine], tile_send.at[slot + 1], tile_recv.at[1],
        {"lat": jnp.maximum(lat - 1, 0), "chan": chan_n - 1},
    )

    local[0].wait()
    pick = one_hot((2 * half_cols, LANES), lambda row, col: row == 2 * col)

    def take_even(i, _):
        picked = lax.dot_general(fbuf[i], pick, (((0,), (0,)), ((), ())), preferred_element_type=F32)
        even_t[:, pl.ds(pl.multiple_of(i * LANES, LANES), LANES)] = picked.astype(BF16)
        return 0

    lax.fori_loop(0, h, take_even, 0)

    @pl.when(is_top)
    def _():
        tiles[0] = jnp.zeros(tiles.shape[1:], BF16)

    @pl.when(is_bottom)
    def _():
        tiles[h + 1] = jnp.zeros(tiles.shape[1:], BF16)

    @pl.when(jnp.logical_not(is_top))
    def _():
        pltpu.make_async_copy(tiles.at[0], tiles.at[0], tile_recv.at[0]).wait()

    @pl.when(jnp.logical_not(is_bottom))
    def _():
        pltpu.make_async_copy(tiles.at[h + 1], tiles.at[h + 1], tile_recv.at[1]).wait()

    pltpu.make_async_copy(tiles.at[pl.ds(1, h)], tiles.at[pl.ds(1, h)], tile_recv.at[2]).wait()

    def shifted_source(row, col):
        s, j = col // LANES, col % LANES
        return jnp.logical_and(row == j + 1 - s, j < half_cols)

    shift = one_hot((half_cols, 3 * LANES), shifted_source)

    def build(k, edges):
        tile = tiles[k]
        moved = jnp.dot(tile, shift, preferred_element_type=F32).astype(BF16)
        at = pl.ds(pl.multiple_of(k * LANES, LANES), LANES)
        for s in range(3):
            taps[pl.ds(s * out_ch, out_ch), at] = moved[:, s * LANES:(s + 1) * LANES]
        last = one_hot(
            (half_cols, 2 * LANES),
            lambda row, col: jnp.logical_or(
                jnp.logical_and(row == half_cols - 1, col == k), jnp.logical_and(row == 0, col == k + LANES)
            ),
        )
        return edges + jnp.dot(tile, last, preferred_element_type=F32)

    edges = lax.fori_loop(0, h + 2, build, jnp.zeros((out_ch, 2 * LANES), F32)).astype(BF16)
    edge_out[0] = edges[:, :LANES]
    edge_out[1] = edges[:, LANES:]
    send(None, edge_out.at[0], edge_in.at[0], edge_send.at[0], edge_recv.at[0], {"lon": other("lon", 1)})
    send(None, edge_out.at[1], edge_in.at[1], edge_send.at[1], edge_recv.at[1], {"lon": other("lon", lon_n - 1)})
    for side in range(2):
        pltpu.make_async_copy(edge_in.at[side], edge_in.at[side], edge_recv.at[side]).wait()

    def inject(k, _):
        at = pl.ds(pl.multiple_of(k * LANES, LANES), LANES)
        for side, s, lane in ((1, 0, half_cols - 1), (0, 2, 0)):
            spot = one_hot((LANES, LANES), lambda row, col: jnp.logical_and(row == k, col == lane))
            block = taps[pl.ds(s * out_ch, out_ch), at].astype(F32)
            block = block + jnp.dot(edge_in[side], spot, preferred_element_type=F32)
            taps[pl.ds(s * out_ch, out_ch), at] = block.astype(BF16)
        return 0

    lax.fori_loop(0, h + 2, inject, 0)

    counter = {"red": 0, "gat": 0, "land": 0}
    blocks = reduce_blocks(acc.shape[0], sizes)
    state = []

    def weight_terms(r):
        part = lax.dot_general(
            even_t[...], taps[:, (2 - r) * LANES:(2 - r + h) * LANES], (((1,), (1,)), ((), ())), preferred_element_type=F32
        )
        for s in range(3):
            acc[pl.ds((3 * r + s) * in_ch, in_ch), :] = part[:, s * out_ch:(s + 1) * out_ch]

    def owner_of(index, axis, owners):
        if owners == sizes[axis]:
            return None, index
        return index < owners, jnp.minimum(index, owners - 1)

    def scatter(block, stage):
        start, plan = blocks[block]
        axis, part, owners = plan[stage]
        base = start if stage == 0 else state[block]["base"]
        if stage == 0:
            state.append({"stack": []})
        land = landing[counter["land"]]
        counter["land"] += 1
        arrivals = []
        for d in range(1, sizes[axis]):
            p = other(axis, d)
            n = counter["red"]
            counter["red"] += 1
            toowner, target = owner_of(p, axis, owners)
            send(
                toowner, acc.at[pl.ds(pl.multiple_of(base + target * part, 8), part)], land.at[d - 1],
                red_send.at[n], red_recv.at[n], {axis: p},
            )
            arrivals.append(n)
        amowner, own = owner_of(me[axis], axis, owners)
        state[block]["base"] = base + own * part
        state[block]["stack"].append((axis, part, owners, base, amowner, own))
        state[block]["open"] = (land, arrivals, amowner, part)

    def add_up(block, final=False):
        land, arrivals, amowner, part = state[block]["open"]
        at = pl.ds(pl.multiple_of(state[block]["base"], 8), part)

        def absorb():
            for position, n in enumerate(arrivals):
                pltpu.make_async_copy(land.at[position], land.at[position], red_recv.at[n]).wait()
            total = acc[at, :]
            for position in range(len(arrivals)):
                total = total + land[position]
            if final:
                kg_out[at, :] = total * scale
            else:
                acc[at, :] = total

        if amowner is None:
            absorb()
        else:
            pl.when(amowner)(absorb)

    def gather(block, stage):
        axis, part, owners, base, amowner, own = state[block]["stack"][stage]
        at = pl.ds(pl.multiple_of(base + own * part, 8), part)
        waits = []
        for d in range(1, sizes[axis]):
            n = counter["gat"]
            counter["gat"] += 1
            send(amowner, kg_out.at[at], kg_out.at[at], gat_send.at[n], gat_recv.at[n], {axis: other(axis, d)})
            fromowner, source = owner_of(other(axis, sizes[axis] - d), axis, owners)
            there = kg_out.at[pl.ds(pl.multiple_of(base + source * part, 8), part)]
            waits.append((fromowner, pltpu.make_async_copy(there, there, gat_recv.at[n])))
        state[block]["waits"] = waits

    def gathered(block):
        for condition, copy in state[block]["waits"]:
            if condition is None:
                copy.wait()
            else:
                pl.when(condition)(lambda copy=copy: copy.wait())

    spread = one_hot((2 * half_cols, LANES), lambda row, col: row == 2 * col)

    def make_even_grad(i, _):
        total = jnp.zeros((in_ch, 2 * LANES), F32)
        for r in range(3):
            at = pl.ds(pl.multiple_of(i * 2 * LANES + (2 - r) * LANES, LANES), 2 * LANES)
            total = total + jnp.dot(kcat[r], taps[:, at], preferred_element_type=F32)
        total = total.astype(BF16)
        for k in range(2):
            row = lax.dot_general(
                spread, total[:, k * LANES:(k + 1) * LANES], (((1,), (1,)), ((), ())), preferred_element_type=F32
            )
            rows_buf[2 * i + k] = row.astype(BF16)
        return 0

    pairs = h // 2
    row_copies = []
    cuts = [pairs * k // 4 for k in range(5)]

    def even_grads(k):
        lax.fori_loop(cuts[k], cuts[k + 1], make_even_grad, 0)
        at = pl.ds(2 * cuts[k], 2 * (cuts[k + 1] - cuts[k]))
        copy = pltpu.make_async_copy(rows_buf.at[at], rows_out.at[at], row_sem.at[k])
        copy.start()
        row_copies.append(copy)

    weight_terms(0)
    scatter(0, 0)
    weight_terms(1)
    add_up(0)
    scatter(0, 1)
    scatter(1, 0)
    weight_terms(2)
    add_up(1)
    scatter(1, 1)
    scatter(2, 0)
    for copy in local[1:]:
        copy.wait()
    add_up(2)
    scatter(2, 1)
    even_grads(0)
    for block in range(3):
        add_up(block)
        scatter(block, 2)
        even_grads(block + 1)
    for block in range(3):
        add_up(block, True)
        gather(block, 2)
    for stage in (1, 0):
        for block in range(3):
            gathered(block)
            gather(block, stage)
    for block in range(3):
        gathered(block)

    for copy in row_copies:
        copy.wait()
    for condition, copy in sends:
        if condition is None:
            copy.wait_send()
        else:
            pl.when(condition)(lambda copy=copy: copy.wait_send())


def reduce_blocks(rows, sizes):
    count = rows // 3
    return [(block * count, stage_plan(count, ("lat", "chan", "lon"), sizes)) for block in range(3)]


def finish_kernel(rows, kg_in, grad_out, kg_out, rows_buf, kg_buf, zeros, sems):
    zero_rows = zeros.shape[0]
    groups = rows.shape[0] // zero_rows
    kg_read = pltpu.make_async_copy(kg_in, kg_buf, sems.at[0])
    kg_write = pltpu.make_async_copy(kg_buf, kg_out, sems.at[1])
    kg_read.start()
    reads, writes = [], [kg_write]
    for k in range(groups):
        at = pl.ds(k * zero_rows, zero_rows)
        reads.append(pltpu.make_async_copy(rows.at[at], rows_buf.at[at], sems.at[2 + 3 * k]))
        reads[k].start()
    zeros[...] = jnp.zeros(zeros.shape, BF16)
    for k in range(groups):
        at = pl.ds(k * zero_rows, zero_rows)
        writes.append(pltpu.make_async_copy(zeros, grad_out.at[at, 1], sems.at[3 + 3 * k]))
        writes[-1].start()
    kg_read.wait()
    kg_write.start()
    for k in range(groups):
        at = pl.ds(k * zero_rows, zero_rows)
        reads[k].wait()
        writes.append(pltpu.make_async_copy(rows_buf.at[at], grad_out.at[at, 0], sems.at[4 + 3 * k]))
        writes[-1].start()
    for copy in writes:
        copy.wait()


def on_device(sizes, fine_act, coarse_grad, kernel):
    fine_rows, fine_cols, in_ch = fine_act.shape
    out_ch = kernel.shape[3]
    h, w = fine_rows // 2, fine_cols // 2
    lon_n, lat_n, chan_n = (sizes[a] for a in AXES)
    scale = 1.0 / math.sqrt(h * lat_n * chan_n * w * lon_n)
    cg = jnp.transpose(coarse_grad, (0, 2, 1))
    fine = fine_act.reshape(h, 2, fine_cols, in_ch)
    blocks = reduce_blocks(9 * in_ch, sizes)
    landing, count = [], 0
    for block, stage in ((0, 0), (0, 1), (1, 0), (1, 1), (2, 0), (2, 1), (0, 2), (1, 2), (2, 2)):
        axis, part, _ = blocks[block][1][stage]
        landing.append(pltpu.VMEM((sizes[axis] - 1, part, out_ch), F32))
        count += sizes[axis] - 1
    dma = pltpu.SemaphoreType.DMA
    vmem = pl.BlockSpec(memory_space=pltpu.VMEM)
    hbm = pl.BlockSpec(memory_space=pltpu.HBM)
    rows, kg = pl.pallas_call(
        functools.partial(grads_kernel, sizes, h, w, out_ch, scale),
        out_shape=(
            jax.ShapeDtypeStruct((h, fine_cols, in_ch), BF16),
            jax.ShapeDtypeStruct((9 * in_ch, out_ch), F32),
        ),
        in_specs=[hbm, hbm, hbm],
        out_specs=(hbm, vmem),
        scratch_shapes=[
            pltpu.VMEM((h, fine_cols, in_ch), BF16),
            pltpu.VMEM((3, in_ch, 3 * out_ch), BF16),
            pltpu.VMEM((h + 2, out_ch, w), BF16),
            pltpu.VMEM((3 * out_ch, (h + 2) * LANES), BF16),
            pltpu.VMEM((in_ch, h * LANES), BF16),
            pltpu.VMEM((2, out_ch, LANES), BF16),
            pltpu.VMEM((2, out_ch, LANES), BF16),
            pltpu.VMEM((9 * in_ch, out_ch), F32),
            pltpu.VMEM((h, fine_cols, in_ch), BF16),
            dma((4,)),
            *landing,
            dma((10,)),
            dma((3,)),
            dma((3 * (chan_n - 1) + 2,)),
            dma((2,)),
            dma((2,)),
            dma((count,)),
            dma((count,)),
            dma((count,)),
            dma((count,)),
        ],
        compiler_params=pltpu.CompilerParams(
            collective_id=0, has_side_effects=True, vmem_limit_bytes=60 * 1024 * 1024
        ),
        name="grads",
    )(fine, cg, kernel)
    zero_rows = math.gcd(h, 8)
    input_grad, kernel_grad = pl.pallas_call(
        finish_kernel,
        out_shape=(
            jax.ShapeDtypeStruct((h, 2, fine_cols, in_ch), BF16),
            jax.ShapeDtypeStruct(kg.shape, F32),
        ),
        in_specs=[hbm, hbm],
        out_specs=(hbm, hbm),
        scratch_shapes=[
            pltpu.VMEM((h, fine_cols, in_ch), BF16),
            pltpu.VMEM(kg.shape, F32),
            pltpu.VMEM((zero_rows, fine_cols, in_ch), BF16),
            dma((2 + 3 * (h // zero_rows),)),
        ],
        compiler_params=pltpu.CompilerParams(vmem_limit_bytes=60 * 1024 * 1024),
        name="finish",
    )(rows, kg)
    return (input_grad.reshape(fine_act.shape), kernel_grad.reshape(3, 3, in_ch, out_ch))


def solution(mesh):
    placed = (P(("parts", "lat", "chan"), "lon", None), P(("parts", "lat"), "lon", "chan"), P())
    sizes = {axis: mesh.shape[axis] for axis in AXES}
    return jax.shard_map(
        functools.partial(on_device, sizes),
        mesh=mesh,
        in_specs=placed,
        out_specs=(P(("parts", "lat", "chan"), "lon", None), P("parts", None, None, None)),
        check_vma=False,
    )
```

```python
import functools
import math

import jax
import jax.numpy as jnp
from jax import lax
from jax.experimental import pallas as pl
from jax.experimental.pallas import tpu as pltpu
from jax.sharding import PartitionSpec as P

MESH = pl.DeviceIdType.MESH
LANES = 128
F32 = jnp.float32
BF16 = jnp.bfloat16
TAP_ORDER = (1, 0, 2)
AXES = ("lon", "lat", "chan")


def one_hot(shape, test):
    rows = lax.broadcasted_iota(jnp.int32, shape, 0)
    cols = lax.broadcasted_iota(jnp.int32, shape, 1)
    return jnp.where(test(rows, cols), 1.0, 0.0).astype(BF16)


def share(rows, peers, unit):
    for size in range(unit, rows + 1, unit):
        if rows % size == 0 and rows // size <= peers:
            return size
    raise ValueError("no share")


def stage_plan(rows, order, sizes):
    plan = []
    for position, axis in enumerate(order):
        unit = 8
        for later in order[position + 1:]:
            unit *= sizes[later] if later != "lon" else 1
        part = share(rows, sizes[axis], unit)
        plan.append((axis, part, rows // part))
        rows = part
    return plan


def grads_kernel(
    sizes, half_rows, half_cols, out_ch, scale,
    fine, cg, kernel, rows_out, kg_out,
    fbuf, kcat, tiles, taps, even_t, edge_out, edge_in, spots, acc, rows_buf, row_sem, *rest,
):
    landing, (local_sem, tile_recv, tile_send, edge_send, edge_recv, red_send, red_recv, gat_send, gat_recv) = rest[:-9], rest[-9:]
    lon_n, lat_n, chan_n = (sizes[a] for a in AXES)
    me = {a: lax.axis_index(a) for a in AXES}
    lat, chan = me["lat"], me["chan"]
    h = half_rows
    group = group_size(h + 2)
    spans = [(max(1, q * group), min(h + 1, (q + 1) * group)) for q in range((h + 2) // group)]
    width = cg.shape[1]
    in_ch = fbuf.shape[2]
    mine = pl.ds(pl.multiple_of(chan * width, width), width)

    def other(axis, step):
        return lax.rem(me[axis] + step, sizes[axis])

    local = [pltpu.make_async_copy(fine.at[:, 0], fbuf, local_sem.at[0])]
    for r in range(3):
        for s in range(3):
            local.append(
                pltpu.make_async_copy(
                    kernel.at[r, s], kcat.at[r, :, pl.ds(s * out_ch, out_ch)], local_sem.at[1 + 3 * r + s]
                )
            )
    for copy in local:
        copy.start()

    is_top = jnp.logical_and(lat == 0, chan == 0)
    is_bottom = jnp.logical_and(lat == lat_n - 1, chan == chan_n - 1)
    for q, (lo, hi) in enumerate(spans):
        pltpu.make_async_copy(
            cg.at[pl.ds(chan * h + lo - 1, hi - lo)], tiles.at[pl.ds(lo, hi - lo), mine], tile_recv.at[2 + q]
        ).start()

    @pl.when(chan > 0)
    def _():
        pltpu.make_async_copy(cg.at[chan * h - 1], tiles.at[0, mine], tile_recv.at[0]).start()

    @pl.when(chan < chan_n - 1)
    def _():
        pltpu.make_async_copy(cg.at[(chan + 1) * h], tiles.at[h + 1, mine], tile_recv.at[1]).start()

    barrier = pltpu.get_barrier_semaphore()
    greeted = 0
    for dl in range(lat_n):
        for dc in range(chan_n):
            if dl or dc:
                pl.semaphore_signal(
                    barrier, inc=1, device_id={"lat": other("lat", dl), "chan": other("chan", dc)}, device_id_type=MESH
                )
                greeted += 1
    for d in range(1, lon_n):
        pl.semaphore_signal(barrier, inc=1, device_id={"lon": other("lon", d)}, device_id_type=MESH)
        greeted += 1
    pl.semaphore_wait(barrier, greeted)

    sends = []

    def send(condition, src, dst, send_sem, recv_sem, where):
        copy = pltpu.make_async_remote_copy(
            src_ref=src, dst_ref=dst, send_sem=send_sem, recv_sem=recv_sem, device_id=where, device_id_type=MESH
        )
        if condition is None:
            copy.start()
        else:
            pl.when(condition)(lambda: copy.start())
        sends.append((condition, copy))

    slot = 0
    for d in range(1, chan_n):
        p = other("chan", d)
        send(p > 0, cg.at[jnp.maximum(p * h - 1, 0)], tiles.at[0, mine], tile_send.at[slot], tile_recv.at[0], {"chan": p})
        slot += 1
    send(
        lat < lat_n - 1, cg.at[chan_n * h - 1], tiles.at[0, mine], tile_send.at[slot], tile_recv.at[0],
        {"lat": jnp.minimum(lat + 1, lat_n - 1), "chan": 0},
    )
    send(
        lat > 0, cg.at[0], tiles.at[h + 1, mine], tile_send.at[slot + 1], tile_recv.at[1],
        {"lat": jnp.maximum(lat - 1, 0), "chan": chan_n - 1},
    )
    slot += 2
    for q, (lo, hi) in enumerate(spans):
        for d in range(1, chan_n):
            p = other("chan", d)
            send(
                None, cg.at[pl.ds(p * h + lo - 1, hi - lo)], tiles.at[pl.ds(lo, hi - lo), mine],
                tile_send.at[slot], tile_recv.at[2 + q], {"chan": p},
            )
            slot += 1
    for d in range(1, chan_n):
        p = other("chan", d)
        send(
            p < chan_n - 1, cg.at[jnp.minimum((p + 1) * h, chan_n * h - 1)], tiles.at[h + 1, mine],
            tile_send.at[slot], tile_recv.at[1], {"chan": p},
        )
        slot += 1

    local[0].wait()
    pick = one_hot((2 * half_cols, LANES), lambda row, col: row == 2 * col)

    def take_even(i, _):
        picked = lax.dot_general(fbuf[i], pick, (((0,), (0,)), ((), ())), preferred_element_type=F32)
        even_t[:, pl.ds(pl.multiple_of(i * LANES, LANES), LANES)] = picked.astype(BF16)
        return 0

    lax.fori_loop(0, h, take_even, 0)

    @pl.when(is_top)
    def _():
        tiles[0] = jnp.zeros(tiles.shape[1:], BF16)

    @pl.when(is_bottom)
    def _():
        tiles[h + 1] = jnp.zeros(tiles.shape[1:], BF16)

    def make_spots(k, _):
        at = pl.ds(pl.multiple_of(k * LANES, LANES), LANES)
        for side, lane in ((0, half_cols - 1), (1, 0)):
            spots[side, :, at] = one_hot((LANES, LANES), lambda row, col: jnp.logical_and(row == k, col == lane))
        return 0

    lax.fori_loop(0, h + 2, make_spots, 0)

    def shifted_source(row, col):
        s, j = col // LANES, col % LANES
        return jnp.logical_and(row == j + 1 - s, j < half_cols)

    shift = one_hot((half_cols, 3 * LANES), shifted_source)

    for q, (lo, hi) in enumerate(spans):
        if q == 0:

            @pl.when(jnp.logical_not(is_top))
            def _():
                pltpu.make_async_copy(tiles.at[0], tiles.at[0], tile_recv.at[0]).wait()

        pltpu.make_async_copy(tiles.at[pl.ds(lo, hi - lo)], tiles.at[pl.ds(lo, hi - lo)], tile_recv.at[2 + q]).wait()
        if q == len(spans) - 1:

            @pl.when(jnp.logical_not(is_bottom))
            def _():
                pltpu.make_async_copy(tiles.at[h + 1], tiles.at[h + 1], tile_recv.at[1]).wait()

        block = tiles[pl.ds(q * group, group)].reshape(group * out_ch, half_cols)
        moved = jnp.dot(block, shift, preferred_element_type=F32).astype(BF16)
        for k in range(group):
            for s in range(3):
                taps[pl.ds(s * out_ch, out_ch), pl.ds((q * group + k) * LANES, LANES)] = moved[
                    k * out_ch:(k + 1) * out_ch, s * LANES:(s + 1) * LANES
                ]

    centre = taps[pl.ds(out_ch, out_ch), :]
    for side in range(2):
        edge_out[side] = lax.dot_general(
            centre, spots[side], (((1,), (1,)), ((), ())), preferred_element_type=F32
        ).astype(BF16)
    send(None, edge_out.at[0], edge_in.at[0], edge_send.at[0], edge_recv.at[0], {"lon": other("lon", 1)})
    send(None, edge_out.at[1], edge_in.at[1], edge_send.at[1], edge_recv.at[1], {"lon": other("lon", lon_n - 1)})

    def inject(s, came, spot):
        pltpu.make_async_copy(edge_in.at[came], edge_in.at[came], edge_recv.at[came]).wait()
        at = pl.ds(s * out_ch, out_ch)
        put = jnp.dot(edge_in[came], spots[spot], preferred_element_type=F32)
        taps[at, :] = (taps[at, :].astype(F32) + put).astype(BF16)

    counter = {"red": 0, "gat": 0, "land": 0}
    blocks = reduce_blocks(acc.shape[0], sizes)
    state = []

    def weight_terms(block):
        s = TAP_ORDER[block]
        for r in range(3):
            acc[pl.ds((3 * block + r) * in_ch, in_ch), :] = lax.dot_general(
                even_t[...], taps[pl.ds(s * out_ch, out_ch), pl.ds((2 - r) * LANES, h * LANES)],
                (((1,), (1,)), ((), ())), preferred_element_type=F32,
            )

    def owner_of(index, axis, owners):
        if owners == sizes[axis]:
            return None, index
        return index < owners, jnp.minimum(index, owners - 1)

    def scatter(block, stage):
        start, plan = blocks[block]
        axis, part, owners = plan[stage]
        base = start if stage == 0 else state[block]["base"]
        if stage == 0:
            state.append({"stack": []})
        land = landing[counter["land"]]
        counter["land"] += 1
        arrivals = []
        for d in range(1, sizes[axis]):
            p = other(axis, d)
            n = counter["red"]
            counter["red"] += 1
            toowner, target = owner_of(p, axis, owners)
            send(
                toowner, acc.at[pl.ds(pl.multiple_of(base + target * part, 8), part)], land.at[d - 1],
                red_send.at[n], red_recv.at[n], {axis: p},
            )
            arrivals.append(n)
        amowner, own = owner_of(me[axis], axis, owners)
        state[block]["base"] = base + own * part
        state[block]["stack"].append((axis, part, owners, base, amowner, own))
        state[block]["open"] = (land, arrivals, amowner, part)

    def add_up(block, final=False):
        land, arrivals, amowner, part = state[block]["open"]
        at = pl.ds(pl.multiple_of(state[block]["base"], 8), part)

        def absorb():
            for position, n in enumerate(arrivals):
                pltpu.make_async_copy(land.at[position], land.at[position], red_recv.at[n]).wait()
            total = acc[at, :]
            for position in range(len(arrivals)):
                total = total + land[position]
            if final:
                kg_out[at, :] = total * scale
            else:
                acc[at, :] = total

        if amowner is None:
            absorb()
        else:
            pl.when(amowner)(absorb)

    def gather(block, stage):
        axis, part, owners, base, amowner, own = state[block]["stack"][stage]
        at = pl.ds(pl.multiple_of(base + own * part, 8), part)
        waits = []
        for d in range(1, sizes[axis]):
            n = counter["gat"]
            counter["gat"] += 1
            send(amowner, kg_out.at[at], kg_out.at[at], gat_send.at[n], gat_recv.at[n], {axis: other(axis, d)})
            fromowner, source = owner_of(other(axis, sizes[axis] - d), axis, owners)
            there = kg_out.at[pl.ds(pl.multiple_of(base + source * part, 8), part)]
            waits.append((fromowner, pltpu.make_async_copy(there, there, gat_recv.at[n])))
        state[block]["waits"] = waits

    def gathered(block):
        for condition, copy in state[block]["waits"]:
            if condition is None:
                copy.wait()
            else:
                pl.when(condition)(lambda copy=copy: copy.wait())

    spread = one_hot((2 * half_cols, LANES), lambda row, col: row == 2 * col)

    def make_even_grad(i, _):
        total = jnp.zeros((in_ch, 2 * LANES), F32)
        for r in range(3):
            at = pl.ds(pl.multiple_of(i * 2 * LANES + (2 - r) * LANES, LANES), 2 * LANES)
            total = total + jnp.dot(kcat[r], taps[:, at], preferred_element_type=F32)
        total = total.astype(BF16)
        for k in range(2):
            row = lax.dot_general(
                spread, total[:, k * LANES:(k + 1) * LANES], (((1,), (1,)), ((), ())), preferred_element_type=F32
            )
            rows_buf[2 * i + k] = row.astype(BF16)
        return 0

    pairs = h // 2
    row_copies = []
    cuts = [pairs * k // 4 for k in range(5)]

    def even_grads(k):
        lax.fori_loop(cuts[k], cuts[k + 1], make_even_grad, 0)
        at = pl.ds(2 * cuts[k], 2 * (cuts[k + 1] - cuts[k]))
        copy = pltpu.make_async_copy(rows_buf.at[at], rows_out.at[at], row_sem.at[k])
        copy.start()
        row_copies.append(copy)

    weight_terms(0)
    scatter(0, 0)
    inject(0, 1, 0)
    add_up(0)
    scatter(0, 1)
    weight_terms(1)
    scatter(1, 0)
    inject(2, 0, 1)
    add_up(1)
    scatter(1, 1)
    weight_terms(2)
    scatter(2, 0)
    for copy in local[1:]:
        copy.wait()
    add_up(2)
    scatter(2, 1)
    even_grads(0)
    for block in range(3):
        add_up(block)
        scatter(block, 2)
        even_grads(block + 1)
    for block in range(3):
        add_up(block, True)
        gather(block, 2)
    for stage in (1, 0):
        for block in range(3):
            gathered(block)
            gather(block, stage)
    for block in range(3):
        gathered(block)

    for copy in row_copies:
        copy.wait()
    for condition, copy in sends:
        if condition is None:
            copy.wait_send()
        else:
            pl.when(condition)(lambda copy=copy: copy.wait_send())


def group_size(slots):
    return max(size for size in range(1, 14) if slots % size == 0)


def reduce_blocks(rows, sizes):
    count = rows // 3
    return [(block * count, stage_plan(count, ("lat", "chan", "lon"), sizes)) for block in range(3)]


def finish_kernel(rows, kg_in, grad_out, kg_out, rows_buf, kg_buf, zeros, sems, kg_sems):
    zero_rows = zeros.shape[0]
    groups = rows.shape[0] // zero_rows
    kg_read = pltpu.make_async_copy(kg_in, kg_buf, sems.at[0])
    in_ch = kg_in.shape[0] // 9
    kg_writes = []
    for block in range(3):
        for r in range(3):
            kg_writes.append(
                pltpu.make_async_copy(
                    kg_buf.at[pl.ds((3 * block + r) * in_ch, in_ch)],
                    kg_out.at[pl.ds((3 * r + TAP_ORDER[block]) * in_ch, in_ch)],
                    kg_sems.at[3 * block + r],
                )
            )
    kg_read.start()
    reads, writes = [], list(kg_writes)
    for k in range(groups):
        at = pl.ds(k * zero_rows, zero_rows)
        reads.append(pltpu.make_async_copy(rows.at[at], rows_buf.at[at], sems.at[2 + 3 * k]))
        reads[k].start()
    zeros[...] = jnp.zeros(zeros.shape, BF16)
    for k in range(groups):
        at = pl.ds(k * zero_rows, zero_rows)
        writes.append(pltpu.make_async_copy(zeros, grad_out.at[at, 1], sems.at[3 + 3 * k]))
        writes[-1].start()
    kg_read.wait()
    for copy in kg_writes:
        copy.start()
    for k in range(groups):
        at = pl.ds(k * zero_rows, zero_rows)
        reads[k].wait()
        writes.append(pltpu.make_async_copy(rows_buf.at[at], grad_out.at[at, 0], sems.at[4 + 3 * k]))
        writes[-1].start()
    for copy in writes:
        copy.wait()


def on_device(sizes, fine_act, coarse_grad, kernel):
    fine_rows, fine_cols, in_ch = fine_act.shape
    out_ch = kernel.shape[3]
    h, w = fine_rows // 2, fine_cols // 2
    lon_n, lat_n, chan_n = (sizes[a] for a in AXES)
    scale = 1.0 / math.sqrt(h * lat_n * chan_n * w * lon_n)
    cg = jnp.transpose(coarse_grad, (0, 2, 1))
    fine = fine_act.reshape(h, 2, fine_cols, in_ch)
    blocks = reduce_blocks(9 * in_ch, sizes)
    landing, count = [], 0
    groups = (h + 2) // group_size(h + 2)
    for block, stage in ((0, 0), (0, 1), (1, 0), (1, 1), (2, 0), (2, 1), (0, 2), (1, 2), (2, 2)):
        axis, part, _ = blocks[block][1][stage]
        landing.append(pltpu.VMEM((sizes[axis] - 1, part, out_ch), F32))
        count += sizes[axis] - 1
    dma = pltpu.SemaphoreType.DMA
    vmem = pl.BlockSpec(memory_space=pltpu.VMEM)
    hbm = pl.BlockSpec(memory_space=pltpu.HBM)
    rows, kg = pl.pallas_call(
        functools.partial(grads_kernel, sizes, h, w, out_ch, scale),
        out_shape=(
            jax.ShapeDtypeStruct((h, fine_cols, in_ch), BF16),
            jax.ShapeDtypeStruct((9 * in_ch, out_ch), F32),
        ),
        in_specs=[hbm, hbm, hbm],
        out_specs=(hbm, vmem),
        scratch_shapes=[
            pltpu.VMEM((h, fine_cols, in_ch), BF16),
            pltpu.VMEM((3, in_ch, 3 * out_ch), BF16),
            pltpu.VMEM((h + 2, out_ch, w), BF16),
            pltpu.VMEM((3 * out_ch, (h + 2) * LANES), BF16),
            pltpu.VMEM((in_ch, h * LANES), BF16),
            pltpu.VMEM((2, out_ch, LANES), BF16),
            pltpu.VMEM((2, out_ch, LANES), BF16),
            pltpu.VMEM((2, LANES, (h + 2) * LANES), BF16),
            pltpu.VMEM((9 * in_ch, out_ch), F32),
            pltpu.VMEM((h, fine_cols, in_ch), BF16),
            dma((4,)),
            *landing,
            dma((10,)),
            dma((2 + groups,)),
            dma(((2 + groups) * (chan_n - 1) + 2,)),
            dma((2,)),
            dma((2,)),
            dma((count,)),
            dma((count,)),
            dma((count,)),
            dma((count,)),
        ],
        compiler_params=pltpu.CompilerParams(
            collective_id=0, has_side_effects=True, vmem_limit_bytes=60 * 1024 * 1024
        ),
        name="grads",
    )(fine, cg, kernel)
    zero_rows = math.gcd(h, 8)
    input_grad, kernel_grad = pl.pallas_call(
        finish_kernel,
        out_shape=(
            jax.ShapeDtypeStruct((h, 2, fine_cols, in_ch), BF16),
            jax.ShapeDtypeStruct(kg.shape, F32),
        ),
        in_specs=[hbm, hbm],
        out_specs=(hbm, hbm),
        scratch_shapes=[
            pltpu.VMEM((h, fine_cols, in_ch), BF16),
            pltpu.VMEM(kg.shape, F32),
            pltpu.VMEM((zero_rows, fine_cols, in_ch), BF16),
            dma((2 + 3 * (h // zero_rows),)),
            dma((9,)),
        ],
        compiler_params=pltpu.CompilerParams(vmem_limit_bytes=60 * 1024 * 1024),
        name="finish",
    )(rows, kg)
    return (input_grad.reshape(fine_act.shape), kernel_grad.reshape(3, 3, in_ch, out_ch))


def solution(mesh):
    placed = (P(("parts", "lat", "chan"), "lon", None), P(("parts", "lat"), "lon", "chan"), P())
    sizes = {axis: mesh.shape[axis] for axis in AXES}
    return jax.shard_map(
        functools.partial(on_device, sizes),
        mesh=mesh,
        in_specs=placed,
        out_specs=(P(("parts", "lat", "chan"), "lon", None), P("parts", None, None, None)),
        check_vma=False,
    )
```

```python
import functools
import math

import jax
import jax.numpy as jnp
from jax import lax
from jax.experimental import pallas as pl
from jax.experimental.pallas import tpu as pltpu
from jax.sharding import PartitionSpec as P

MESH = pl.DeviceIdType.MESH
LANES = 128
F32 = jnp.float32
BF16 = jnp.bfloat16
TAP_ORDER = (1, 0, 2)
AXES = ("lon", "lat", "chan")


def one_hot(shape, test):
    rows = lax.broadcasted_iota(jnp.int32, shape, 0)
    cols = lax.broadcasted_iota(jnp.int32, shape, 1)
    return jnp.where(test(rows, cols), 1.0, 0.0).astype(BF16)


def share(rows, peers, unit):
    for size in range(unit, rows + 1, unit):
        if rows % size == 0 and rows // size <= peers:
            return size
    raise ValueError("no share")


def stage_plan(rows, order, sizes):
    plan = []
    for position, axis in enumerate(order):
        unit = 8
        for later in order[position + 1:]:
            unit *= sizes[later] if later != "lon" else 1
        part = share(rows, sizes[axis], unit)
        plan.append((axis, part, rows // part))
        rows = part
    return plan


def grads_kernel(
    sizes, half_rows, half_cols, out_ch, scale,
    fine, cg, kernel, rows_out, kg_out,
    fbuf, kcat, tiles, taps, even_t, edge_out, edge_in, spots, acc, rows_buf, row_sem, *rest,
):
    landing, (local_sem, tile_recv, tile_send, edge_send, edge_recv, red_send, red_recv, gat_send, gat_recv) = rest[:-9], rest[-9:]
    lon_n, lat_n, chan_n = (sizes[a] for a in AXES)
    me = {a: lax.axis_index(a) for a in AXES}
    lat, chan = me["lat"], me["chan"]
    h = half_rows
    group = group_size(h + 2)
    spans = [(max(1, q * group), min(h + 1, (q + 1) * group)) for q in range((h + 2) // group)]
    width = cg.shape[1]
    in_ch = fbuf.shape[2]
    mine = pl.ds(pl.multiple_of(chan * width, width), width)

    def other(axis, step):
        return lax.rem(me[axis] + step, sizes[axis])

    local = [pltpu.make_async_copy(fine.at[:, 0], fbuf, local_sem.at[0])]
    for r in range(3):
        for s in range(3):
            local.append(
                pltpu.make_async_copy(
                    kernel.at[r, s], kcat.at[r, :, pl.ds(s * out_ch, out_ch)], local_sem.at[1 + 3 * r + s]
                )
            )
    for copy in local:
        copy.start()

    is_top = jnp.logical_and(lat == 0, chan == 0)
    is_bottom = jnp.logical_and(lat == lat_n - 1, chan == chan_n - 1)
    for q, (lo, hi) in enumerate(spans):
        pltpu.make_async_copy(
            cg.at[pl.ds(chan * h + lo - 1, hi - lo)], tiles.at[pl.ds(lo, hi - lo), mine], tile_recv.at[2 + q]
        ).start()

    @pl.when(chan > 0)
    def _():
        pltpu.make_async_copy(cg.at[chan * h - 1], tiles.at[0, mine], tile_recv.at[0]).start()

    @pl.when(chan < chan_n - 1)
    def _():
        pltpu.make_async_copy(cg.at[(chan + 1) * h], tiles.at[h + 1, mine], tile_recv.at[1]).start()

    barrier = pltpu.get_barrier_semaphore()
    greeted = 0
    for dl in range(lat_n):
        for dc in range(chan_n):
            if dl or dc:
                pl.semaphore_signal(
                    barrier, inc=1, device_id={"lat": other("lat", dl), "chan": other("chan", dc)}, device_id_type=MESH
                )
                greeted += 1
    for d in range(1, lon_n):
        pl.semaphore_signal(barrier, inc=1, device_id={"lon": other("lon", d)}, device_id_type=MESH)
        greeted += 1
    pl.semaphore_wait(barrier, greeted)

    sends = []

    def send(condition, src, dst, send_sem, recv_sem, where):
        copy = pltpu.make_async_remote_copy(
            src_ref=src, dst_ref=dst, send_sem=send_sem, recv_sem=recv_sem, device_id=where, device_id_type=MESH
        )
        if condition is None:
            copy.start()
        else:
            pl.when(condition)(lambda: copy.start())
        sends.append((condition, copy))

    slot = 0
    for d in range(1, chan_n):
        p = other("chan", d)
        send(p > 0, cg.at[jnp.maximum(p * h - 1, 0)], tiles.at[0, mine], tile_send.at[slot], tile_recv.at[0], {"chan": p})
        slot += 1
    send(
        lat < lat_n - 1, cg.at[chan_n * h - 1], tiles.at[0, mine], tile_send.at[slot], tile_recv.at[0],
        {"lat": jnp.minimum(lat + 1, lat_n - 1), "chan": 0},
    )
    send(
        lat > 0, cg.at[0], tiles.at[h + 1, mine], tile_send.at[slot + 1], tile_recv.at[1],
        {"lat": jnp.maximum(lat - 1, 0), "chan": chan_n - 1},
    )
    slot += 2
    for q, (lo, hi) in enumerate(spans):
        for d in range(1, chan_n):
            p = other("chan", d)
            send(
                None, cg.at[pl.ds(p * h + lo - 1, hi - lo)], tiles.at[pl.ds(lo, hi - lo), mine],
                tile_send.at[slot], tile_recv.at[2 + q], {"chan": p},
            )
            slot += 1
    for d in range(1, chan_n):
        p = other("chan", d)
        send(
            p < chan_n - 1, cg.at[jnp.minimum((p + 1) * h, chan_n * h - 1)], tiles.at[h + 1, mine],
            tile_send.at[slot], tile_recv.at[1], {"chan": p},
        )
        slot += 1

    local[0].wait()
    pick = one_hot((2 * half_cols, LANES), lambda row, col: row == 2 * col)

    def take_even(i, _):
        picked = lax.dot_general(fbuf[i], pick, (((0,), (0,)), ((), ())), preferred_element_type=F32)
        even_t[:, pl.ds(pl.multiple_of(i * LANES, LANES), LANES)] = picked.astype(BF16)
        return 0

    lax.fori_loop(0, h, take_even, 0)

    @pl.when(is_top)
    def _():
        tiles[0] = jnp.zeros(tiles.shape[1:], BF16)

    @pl.when(is_bottom)
    def _():
        tiles[h + 1] = jnp.zeros(tiles.shape[1:], BF16)

    def make_spots(k, _):
        at = pl.ds(pl.multiple_of(k * LANES, LANES), LANES)
        for side, lane in ((0, half_cols - 1), (1, 0)):
            spots[side, :, at] = one_hot((LANES, LANES), lambda row, col: jnp.logical_and(row == k, col == lane))
        return 0

    lax.fori_loop(0, h + 2, make_spots, 0)

    def shifted_source(row, col):
        s, j = col // LANES, col % LANES
        return jnp.logical_and(row == j + 1 - s, j < half_cols)

    shift = one_hot((half_cols, 3 * LANES), shifted_source)

    for q, (lo, hi) in enumerate(spans):
        if q == 0:

            @pl.when(jnp.logical_not(is_top))
            def _():
                pltpu.make_async_copy(tiles.at[0], tiles.at[0], tile_recv.at[0]).wait()

        pltpu.make_async_copy(tiles.at[pl.ds(lo, hi - lo)], tiles.at[pl.ds(lo, hi - lo)], tile_recv.at[2 + q]).wait()
        if q == len(spans) - 1:

            @pl.when(jnp.logical_not(is_bottom))
            def _():
                pltpu.make_async_copy(tiles.at[h + 1], tiles.at[h + 1], tile_recv.at[1]).wait()

        block = tiles[pl.ds(q * group, group)].reshape(group * out_ch, half_cols)
        moved = jnp.dot(block, shift, preferred_element_type=F32).astype(BF16)
        for k in range(group):
            for s in range(3):
                taps[pl.ds(s * out_ch, out_ch), pl.ds((q * group + k) * LANES, LANES)] = moved[
                    k * out_ch:(k + 1) * out_ch, s * LANES:(s + 1) * LANES
                ]

    centre = taps[pl.ds(out_ch, out_ch), :]
    for side in range(2):
        edge_out[side] = lax.dot_general(
            centre, spots[side], (((1,), (1,)), ((), ())), preferred_element_type=F32
        ).astype(BF16)
    send(None, edge_out.at[0], edge_in.at[0], edge_send.at[0], edge_recv.at[0], {"lon": other("lon", 1)})
    send(None, edge_out.at[1], edge_in.at[1], edge_send.at[1], edge_recv.at[1], {"lon": other("lon", lon_n - 1)})

    def inject(s, came, spot):
        pltpu.make_async_copy(edge_in.at[came], edge_in.at[came], edge_recv.at[came]).wait()
        at = pl.ds(s * out_ch, out_ch)
        put = jnp.dot(edge_in[came], spots[spot], preferred_element_type=F32)
        taps[at, :] = (taps[at, :].astype(F32) + put).astype(BF16)

    counter = {"red": 0, "gat": 0, "land": 0}
    blocks = reduce_blocks(acc.shape[0], sizes)
    state = []

    def weight_terms(block):
        s = TAP_ORDER[block]
        for r in range(3):
            acc[pl.ds((3 * block + r) * in_ch, in_ch), :] = lax.dot_general(
                even_t[...], taps[pl.ds(s * out_ch, out_ch), pl.ds((2 - r) * LANES, h * LANES)],
                (((1,), (1,)), ((), ())), preferred_element_type=F32,
            )

    def owner_of(index, axis, owners):
        if owners == sizes[axis]:
            return None, index
        return index < owners, jnp.minimum(index, owners - 1)

    def scatter(block, stage):
        start, plan = blocks[block]
        axis, part, owners = plan[stage]
        base = start if stage == 0 else state[block]["base"]
        if stage == 0:
            state.append({"stack": []})
        land = landing[counter["land"]]
        counter["land"] += 1
        arrivals = []
        for d in range(1, sizes[axis]):
            p = other(axis, d)
            n = counter["red"]
            counter["red"] += 1
            toowner, target = owner_of(p, axis, owners)
            send(
                toowner, acc.at[pl.ds(pl.multiple_of(base + target * part, 8), part)], land.at[d - 1],
                red_send.at[n], red_recv.at[n], {axis: p},
            )
            arrivals.append(n)
        amowner, own = owner_of(me[axis], axis, owners)
        state[block]["base"] = base + own * part
        state[block]["stack"].append((axis, part, owners, base, amowner, own))
        state[block]["open"] = (land, arrivals, amowner, part)

    def add_up(block, final=False):
        land, arrivals, amowner, part = state[block]["open"]
        at = pl.ds(pl.multiple_of(state[block]["base"], 8), part)

        def absorb():
            for position, n in enumerate(arrivals):
                pltpu.make_async_copy(land.at[position], land.at[position], red_recv.at[n]).wait()
            total = acc[at, :]
            for position in range(len(arrivals)):
                total = total + land[position]
            if final:
                kg_out[at, :] = total * scale
            else:
                acc[at, :] = total

        if amowner is None:
            absorb()
        else:
            pl.when(amowner)(absorb)

    def gather(block, stage):
        axis, part, owners, base, amowner, own = state[block]["stack"][stage]
        at = pl.ds(pl.multiple_of(base + own * part, 8), part)
        waits = []
        for d in range(1, sizes[axis]):
            n = counter["gat"]
            counter["gat"] += 1
            send(amowner, kg_out.at[at], kg_out.at[at], gat_send.at[n], gat_recv.at[n], {axis: other(axis, d)})
            fromowner, source = owner_of(other(axis, sizes[axis] - d), axis, owners)
            there = kg_out.at[pl.ds(pl.multiple_of(base + source * part, 8), part)]
            waits.append((fromowner, pltpu.make_async_copy(there, there, gat_recv.at[n])))
        state[block]["waits"] = waits

    def gathered(block):
        for condition, copy in state[block]["waits"]:
            if condition is None:
                copy.wait()
            else:
                pl.when(condition)(lambda copy=copy: copy.wait())

    spread = one_hot((2 * half_cols, LANES), lambda row, col: row == 2 * col)

    def make_even_grad(i, _):
        total = jnp.zeros((in_ch, 2 * LANES), F32)
        for r in range(3):
            at = pl.ds(pl.multiple_of(i * 2 * LANES + (2 - r) * LANES, LANES), 2 * LANES)
            total = total + jnp.dot(kcat[r], taps[:, at], preferred_element_type=F32)
        total = total.astype(BF16)
        for k in range(2):
            row = lax.dot_general(
                spread, total[:, k * LANES:(k + 1) * LANES], (((1,), (1,)), ((), ())), preferred_element_type=F32
            )
            rows_buf[2 * i + k] = row.astype(BF16)
        return 0

    pairs = h // 2
    row_copies = []
    cuts = [pairs * k // 4 for k in range(5)]

    def even_grads(k):
        lax.fori_loop(cuts[k], cuts[k + 1], make_even_grad, 0)
        at = pl.ds(2 * cuts[k], 2 * (cuts[k + 1] - cuts[k]))
        copy = pltpu.make_async_copy(rows_buf.at[at], rows_out.at[at], row_sem.at[k])
        copy.start()
        row_copies.append(copy)

    weight_terms(0)
    scatter(0, 0)
    inject(0, 1, 0)
    add_up(0)
    scatter(0, 1)
    weight_terms(1)
    scatter(1, 0)
    inject(2, 0, 1)
    add_up(1)
    scatter(1, 1)
    add_up(0)
    scatter(0, 2)
    weight_terms(2)
    scatter(2, 0)
    for copy in local[1:]:
        copy.wait()
    add_up(2)
    scatter(2, 1)
    add_up(1)
    scatter(1, 2)
    even_grads(0)
    add_up(2)
    scatter(2, 2)
    for block in range(3):
        even_grads(block + 1)
        add_up(block, True)
        gather(block, 2)
    for stage in (1, 0):
        for block in range(3):
            gathered(block)
            gather(block, stage)
    for block in range(3):
        gathered(block)

    for copy in row_copies:
        copy.wait()
    for condition, copy in sends:
        if condition is None:
            copy.wait_send()
        else:
            pl.when(condition)(lambda copy=copy: copy.wait_send())


def group_size(slots):
    return max(size for size in range(1, 14) if slots % size == 0)


def reduce_blocks(rows, sizes):
    count = rows // 3
    return [(block * count, stage_plan(count, ("lat", "chan", "lon"), sizes)) for block in range(3)]


def finish_kernel(rows, kg_in, grad_out, kg_out, rows_buf, kg_buf, zeros, sems, kg_sems):
    zero_rows = zeros.shape[0]
    groups = rows.shape[0] // zero_rows
    kg_read = pltpu.make_async_copy(kg_in, kg_buf, sems.at[0])
    in_ch = kg_in.shape[0] // 9
    kg_writes = []
    for block in range(3):
        for r in range(3):
            kg_writes.append(
                pltpu.make_async_copy(
                    kg_buf.at[pl.ds((3 * block + r) * in_ch, in_ch)],
                    kg_out.at[pl.ds((3 * r + TAP_ORDER[block]) * in_ch, in_ch)],
                    kg_sems.at[3 * block + r],
                )
            )
    kg_read.start()
    reads, writes = [], list(kg_writes)
    for k in range(groups):
        at = pl.ds(k * zero_rows, zero_rows)
        reads.append(pltpu.make_async_copy(rows.at[at], rows_buf.at[at], sems.at[2 + 3 * k]))
        reads[k].start()
    zeros[...] = jnp.zeros(zeros.shape, BF16)
    for k in range(groups):
        at = pl.ds(k * zero_rows, zero_rows)
        writes.append(pltpu.make_async_copy(zeros, grad_out.at[at, 1], sems.at[3 + 3 * k]))
        writes[-1].start()
    kg_read.wait()
    for copy in kg_writes:
        copy.start()
    for k in range(groups):
        at = pl.ds(k * zero_rows, zero_rows)
        reads[k].wait()
        writes.append(pltpu.make_async_copy(rows_buf.at[at], grad_out.at[at, 0], sems.at[4 + 3 * k]))
        writes[-1].start()
    for copy in writes:
        copy.wait()


def on_device(sizes, fine_act, coarse_grad, kernel):
    fine_rows, fine_cols, in_ch = fine_act.shape
    out_ch = kernel.shape[3]
    h, w = fine_rows // 2, fine_cols // 2
    lon_n, lat_n, chan_n = (sizes[a] for a in AXES)
    scale = 1.0 / math.sqrt(h * lat_n * chan_n * w * lon_n)
    cg = jnp.transpose(coarse_grad, (0, 2, 1))
    fine = fine_act.reshape(h, 2, fine_cols, in_ch)
    blocks = reduce_blocks(9 * in_ch, sizes)
    landing, count = [], 0
    groups = (h + 2) // group_size(h + 2)
    for block, stage in ((0, 0), (0, 1), (1, 0), (1, 1), (0, 2), (2, 0), (2, 1), (1, 2), (2, 2)):
        axis, part, _ = blocks[block][1][stage]
        landing.append(pltpu.VMEM((sizes[axis] - 1, part, out_ch), F32))
        count += sizes[axis] - 1
    dma = pltpu.SemaphoreType.DMA
    vmem = pl.BlockSpec(memory_space=pltpu.VMEM)
    hbm = pl.BlockSpec(memory_space=pltpu.HBM)
    rows, kg = pl.pallas_call(
        functools.partial(grads_kernel, sizes, h, w, out_ch, scale),
        out_shape=(
            jax.ShapeDtypeStruct((h, fine_cols, in_ch), BF16),
            jax.ShapeDtypeStruct((9 * in_ch, out_ch), F32),
        ),
        in_specs=[hbm, hbm, hbm],
        out_specs=(hbm, vmem),
        scratch_shapes=[
            pltpu.VMEM((h, fine_cols, in_ch), BF16),
            pltpu.VMEM((3, in_ch, 3 * out_ch), BF16),
            pltpu.VMEM((h + 2, out_ch, w), BF16),
            pltpu.VMEM((3 * out_ch, (h + 2) * LANES), BF16),
            pltpu.VMEM((in_ch, h * LANES), BF16),
            pltpu.VMEM((2, out_ch, LANES), BF16),
            pltpu.VMEM((2, out_ch, LANES), BF16),
            pltpu.VMEM((2, LANES, (h + 2) * LANES), BF16),
            pltpu.VMEM((9 * in_ch, out_ch), F32),
            pltpu.VMEM((h, fine_cols, in_ch), BF16),
            dma((4,)),
            *landing,
            dma((10,)),
            dma((2 + groups,)),
            dma(((2 + groups) * (chan_n - 1) + 2,)),
            dma((2,)),
            dma((2,)),
            dma((count,)),
            dma((count,)),
            dma((count,)),
            dma((count,)),
        ],
        compiler_params=pltpu.CompilerParams(
            collective_id=0, has_side_effects=True, vmem_limit_bytes=60 * 1024 * 1024
        ),
        name="grads",
    )(fine, cg, kernel)
    zero_rows = math.gcd(h, 8)
    input_grad, kernel_grad = pl.pallas_call(
        finish_kernel,
        out_shape=(
            jax.ShapeDtypeStruct((h, 2, fine_cols, in_ch), BF16),
            jax.ShapeDtypeStruct(kg.shape, F32),
        ),
        in_specs=[hbm, hbm],
        out_specs=(hbm, hbm),
        scratch_shapes=[
            pltpu.VMEM((h, fine_cols, in_ch), BF16),
            pltpu.VMEM(kg.shape, F32),
            pltpu.VMEM((zero_rows, fine_cols, in_ch), BF16),
            dma((2 + 3 * (h // zero_rows),)),
            dma((9,)),
        ],
        compiler_params=pltpu.CompilerParams(vmem_limit_bytes=60 * 1024 * 1024),
        name="finish",
    )(rows, kg)
    return (input_grad.reshape(fine_act.shape), kernel_grad.reshape(3, 3, in_ch, out_ch))


def solution(mesh):
    placed = (P(("parts", "lat", "chan"), "lon", None), P(("parts", "lat"), "lon", "chan"), P())
    sizes = {axis: mesh.shape[axis] for axis in AXES}
    return jax.shard_map(
        functools.partial(on_device, sizes),
        mesh=mesh,
        in_specs=placed,
        out_specs=(P(("parts", "lat", "chan"), "lon", None), P("parts", None, None, None)),
        check_vma=False,
    )
```
